32 devices in a mesh: fsdp: 8 (over y, x, core), tensor: 4 (over z).
Axes of the slice: x: 2, y: 2, z: 4, core: 2. Of those that a mesh axis runs over, the one named last changes fastest.
Arguments:
- tokens: bfloat16 [8192, 4096], P('fsdp'), may hold values from -6 to 6
- input_source: float32 [256, 16, 4096], P('tensor', None, 'fsdp'), may hold values from -0.09375 to 0.09375
- branch_source: float32 [256, 16, 4096], P('tensor', None, 'fsdp'), may hold values from -0.09375 to 0.09375
- output_source: float32 [256, 16, 4096], P('tensor', None, 'fsdp'), may hold values from -0.09375 to 0.09375
- gates_source: float32 [2, 16, 256, 256], P(None, None, 'fsdp', 'tensor'), may hold values from -0.375 to 0.375
- decay_param: float32 [16, 256], replicated, may hold values from -9 to 1
- block_order: int32 [16], replicated, may hold values from 0 to 15, each once
Outputs:
- mixed: bfloat16 [8192, 4096], P('fsdp', 'tensor')
- input_serve: bfloat16 [4096, 4096], P(None, 'tensor')
- branch_serve: bfloat16 [4096, 4096], P(None, 'tensor')
- output_serve: bfloat16 [4096, 4096], P(None, 'tensor')
- gates_serve: bfloat16 [2, 16, 256, 256], P(None, 'tensor')
The draws below stay inside these ranges and needn't reach their ends.
Inputs may be any that keep to these rules, and one draw needn't show every extreme that they name: `block_order`: every gate block appears exactly once.
All inputs are finite; a program needn't handle non-finite values.
Results may differ from the reference program's by a relative error of at most 0.013.
Values may be sent and summed in bfloat16 or wider, within the bound.
A program may use at most 128 MiB of HBM per device.

```python
import jax
import jax.numpy as jnp
from jax import lax

D = 4096
BLOCKS = 16
CHAN = 256
W = 4096
LEN = 256
TOK_DEV = 1024
TOKENS = 8192
N_TENSOR = 4


def shard_levels(rng, shape, cuts, least, largest):
    gain, own = 1.0, jax.random.fold_in(rng, 6)
    for dim, parts in cuts:
        steps = jnp.exp(jax.random.uniform(jax.random.fold_in(own, dim), (parts,), jnp.float32, least / len(cuts), largest / len(cuts)))
        gain = gain * jnp.repeat(steps, shape[dim] // parts).reshape([-1 if axis == dim else 1 for axis in range(len(shape))])
    return gain


def bell_draw(own_key, shape, scale, bound, cuts=(), held_as=jnp.bfloat16):
    level = shard_levels(own_key, shape, cuts, -0.22, 0.18) if cuts else 1.0
    entries = jax.random.normal(own_key, shape, jnp.float32) * scale * level
    return jnp.minimum(jnp.maximum(entries, -bound), bound).astype(held_as)


def setup_inputs(seed: int = 0) -> dict:
    key_of = jax.random.split(jax.random.key(seed), 8)
    tokens = bell_draw(key_of[0], (TOKENS, D), 1.0, 6.0, ((0, 8),))
    input_source = bell_draw(key_of[1], (CHAN, BLOCKS, D), D ** -0.5, 0.09375, ((0, 4), (2, 8)), jnp.float32)
    branch_source = bell_draw(key_of[2], (CHAN, BLOCKS, D), D ** -0.5, 0.09375, ((0, 4), (2, 8)), jnp.float32)
    output_source = bell_draw(key_of[3], (CHAN, BLOCKS, D), W ** -0.5, 0.09375, ((0, 4), (2, 8)), jnp.float32)
    gates_source = bell_draw(key_of[4], (2, BLOCKS, CHAN, CHAN), CHAN ** -0.5, 0.375, ((2, 8), (3, 4)), jnp.float32)
    decay_param = jnp.clip(jax.random.uniform(key_of[5], (BLOCKS, CHAN), jnp.float32, -9.0, 1.0), -9.0, 1.0)
    block_order = jax.random.permutation(key_of[6], BLOCKS).astype(jnp.int32)
    return {"tokens": tokens, "input_source": input_source, "branch_source": branch_source, "output_source": output_source, "gates_source": gates_source, "decay_param": decay_param, "block_order": block_order}


def serving_matrix(source, block_order):
    picked = jnp.take(source, block_order, axis=1)
    return jnp.transpose(picked, (2, 1, 0)).reshape(D, BLOCKS * CHAN).astype(jnp.bfloat16)

def combine_steps(earlier, latter):
    return (earlier[0] * latter[0], latter[0] * earlier[1] + latter[1])

def recurrence(features, input_serve, branch_serve, gates_serve, decay_rows):
    row_count = features.shape[0]
    branch_in = jnp.dot(features, input_serve, preferred_element_type=jnp.float32).astype(jnp.bfloat16)
    gate_pre = jnp.dot(features, branch_serve, preferred_element_type=jnp.float32)
    branch_wide = branch_in.astype(jnp.float32)
    blocked = branch_wide.reshape(row_count, BLOCKS, CHAN)
    gate_table = gates_serve.astype(jnp.float32)
    recur_pre = jnp.einsum('tbi,boi->tbo', blocked, gate_table[0]).reshape(row_count, -1)
    input_pre = jnp.einsum('tbi,boi->tbo', blocked, gate_table[1]).reshape(row_count, -1)
    recur_gate = jax.nn.sigmoid(recur_pre)
    input_gate = jax.nn.sigmoid(input_pre)
    log_decay = -8.0 * jax.nn.softplus(decay_rows) * recur_gate
    decay_step = jnp.exp(log_decay)
    drive_term = jnp.sqrt(1.0 - jnp.exp(2.0 * log_decay)) * (input_gate * branch_wide)
    replicas = row_count // TOK_DEV
    prompts = TOK_DEV // LEN
    shaped = (decay_step.reshape(replicas, LEN, prompts, -1), drive_term.reshape(replicas, LEN, prompts, -1))
    _, states = lax.associative_scan(combine_steps, shaped, axis=1)
    states = states.reshape(row_count, -1)
    return (states * jax.nn.gelu(gate_pre, approximate=True)).astype(jnp.bfloat16)

def reference(tokens, input_source, branch_source, output_source, gates_source, decay_param, block_order):
    input_serve = serving_matrix(input_source, block_order)
    branch_serve = serving_matrix(branch_source, block_order)
    output_serve = serving_matrix(output_source, block_order)
    gates_serve = jnp.transpose(jnp.take(gates_source, block_order, axis=1), (0, 1, 3, 2)).astype(jnp.bfloat16)
    decay_rows = jnp.take(decay_param, block_order, axis=0).reshape(BLOCKS * CHAN)
    gated = recurrence(tokens, input_serve, branch_serve, gates_serve, decay_rows)
    col_width = BLOCKS * CHAN // N_TENSOR
    running = jnp.zeros((tokens.shape[0], D), jnp.float32)
    for tp_group in range(N_TENSOR):
        lower = tp_group * col_width
        partial_value = jnp.dot(gated[:, lower:lower + col_width], output_serve[:, lower:lower + col_width].T, preferred_element_type=jnp.float32)
        rounded = lax.optimization_barrier(partial_value.astype(jnp.bfloat16))
        running = running + rounded.astype(jnp.float32)
    return (running.astype(jnp.bfloat16), input_serve, branch_serve, output_serve, gates_serve)
```

```python
import functools
import jax
import jax.numpy as jnp
from jax import lax
from jax.experimental import pallas as pl
from jax.experimental.pallas import tpu as pltpu
from jax.sharding import PartitionSpec as P

LEN = 256
SUB = 8


def for_sending(shard):
    return jax.tree.map(lambda a: a.astype(jnp.bfloat16) if a.dtype == jnp.float32 else a, shard)


def recur_body(prompts, x_ref, pre_ref, g_ref, r_ref, o_ref, a_s, d_s, carry):
    @pl.when(pl.program_id(1) == 0)
    def _():
        carry[...] = jnp.zeros_like(carry)

    dims = (((1,), (1,)), ((), ()))
    x = x_ref[...]
    pre_r = lax.dot_general(x, g_ref[0, 0], dims, preferred_element_type=jnp.float32)
    pre_i = lax.dot_general(x, g_ref[1, 0], dims, preferred_element_type=jnp.float32)
    a = jnp.exp(r_ref[0] * jax.nn.sigmoid(pre_r))
    a_s[...] = a
    d_s[...] = jnp.sqrt(jnp.maximum(1.0 - a * a, 0.0)) * (
        jax.nn.sigmoid(pre_i) * x.astype(jnp.float32)
    )
    rows, chan = a_s.shape
    group = lax.broadcasted_iota(jnp.int32, (SUB, chan), 0) // prompts

    def last(v):
        res = v
        for g in range(SUB // prompts - 1):
            res = jnp.where(group == g, pltpu.roll(v, (g + 1) * prompts, 0), res)
        return res

    def step(i, c):
        at = pl.ds(pl.multiple_of(i * SUB, SUB), SUB)
        a = a_s[at, :]
        d = d_s[at, :]
        shift = 1
        while shift < SUB // prompts:
            a_sh = pltpu.roll(a, shift * prompts, 0)
            d_sh = pltpu.roll(d, shift * prompts, 0)
            d = jnp.where(group >= shift, a * d_sh + d, d)
            a = jnp.where(group >= shift, a * a_sh, a)
            shift *= 2
        d_s[at, :] = a * c + d
        return last(a) * c + last(d)

    carry[...] = lax.fori_loop(0, rows // SUB, step, carry[...], unroll=8)
    o_ref[...] = (d_s[...] * jax.nn.gelu(pre_ref[...], approximate=True)).astype(o_ref.dtype)


def recur(branch_in, gate_pre, gates, rate, prompts):
    rows, width = branch_in.shape
    blocks, chan = gates.shape[1], gates.shape[2]
    tile = min(rows, 256)
    return pl.pallas_call(
        functools.partial(recur_body, prompts),
        grid=(blocks, rows // tile),
        in_specs=[
            pl.BlockSpec((tile, chan), lambda b, t: (t, b)),
            pl.BlockSpec((tile, chan), lambda b, t: (t, b)),
            pl.BlockSpec((2, 1, chan, chan), lambda b, t: (0, b, 0, 0)),
            pl.BlockSpec((1, 1, chan), lambda b, t: (b, 0, 0)),
        ],
        out_specs=pl.BlockSpec((tile, chan), lambda b, t: (t, b)),
        out_shape=jax.ShapeDtypeStruct((rows, width), jnp.bfloat16),
        scratch_shapes=[
            pltpu.VMEM((tile, chan), jnp.float32),
            pltpu.VMEM((tile, chan), jnp.float32),
            pltpu.VMEM((SUB, chan), jnp.float32),
        ],
        compiler_params=pltpu.CompilerParams(dimension_semantics=("arbitrary", "arbitrary")),
        cost_estimate=pl.CostEstimate(
            flops=4 * rows * width * chan, bytes_accessed=8 * rows * width, transcendentals=6 * rows * width
        ),
        name="recur",
    )(branch_in, gate_pre, gates, rate)


def on_device(
    tokens, input_source, branch_source, output_source, gates_source, decay_param, block_order
):
    tensor_count = lax.axis_size("tensor")
    per_dev = block_order.shape[0] // tensor_count
    own_blocks = lax.dynamic_slice_in_dim(block_order, lax.axis_index("tensor") * per_dev, per_dev)
    casted = (
        input_source.astype(jnp.bfloat16),
        branch_source.astype(jnp.bfloat16),
        output_source.astype(jnp.bfloat16),
    )
    gate_cast = gates_source.astype(jnp.bfloat16)
    sectioned = tuple((jnp.take(weight, block_order, axis=1) for weight in casted))
    regrouped = jax.tree.map(
        lambda part, own: part.astype(own.dtype),
        lax.all_to_all(for_sending(sectioned), "tensor", split_axis=1, concat_axis=0, tiled=True),
        sectioned,
    )
    gate_sectioned = jnp.take(gate_cast, block_order, axis=1)
    gate_group = lax.all_to_all(gate_sectioned, "tensor", split_axis=1, concat_axis=3, tiled=True)
    pieces = tuple(
        (jnp.transpose(weight, (2, 1, 0)).reshape(weight.shape[2], -1) for weight in regrouped)
    )
    gate_piece = jnp.transpose(gate_group, (0, 1, 3, 2))
    gates_serve = lax.all_gather(gate_piece, "fsdp", axis=3, tiled=True)
    row_count = tokens.shape[0]
    input_serve = lax.all_gather(pieces[0], "fsdp", axis=0, tiled=True)
    branch_serve = lax.all_gather(pieces[1], "fsdp", axis=0, tiled=True)
    output_serve = lax.all_gather(pieces[2], "fsdp", axis=0, tiled=True)
    rate = -8.0 * jax.nn.softplus(jnp.take(decay_param, own_blocks, axis=0))[:, None, :]
    branch_in = jnp.dot(tokens, input_serve, preferred_element_type=jnp.float32).astype(jnp.bfloat16)
    gate_pre = jnp.dot(tokens, branch_serve, preferred_element_type=jnp.float32)
    gated = recur(branch_in, gate_pre, gates_serve, rate, row_count // LEN)
    parts = []
    for rows in jnp.split(gated, 2, axis=0):
        partial_value = lax.dot_general(
            rows, output_serve, (((1,), (1,)), ((), ())), preferred_element_type=jnp.float32
        )
        parts.append(
            lax.psum_scatter(
                partial_value.astype(jnp.bfloat16), "tensor", scatter_dimension=1, tiled=True
            )
        )
    mixed = jnp.concatenate(parts, axis=0)
    return (mixed, input_serve, branch_serve, output_serve, gates_serve)


def solution(mesh):
    return jax.shard_map(
        on_device,
        mesh=mesh,
        in_specs=(
            P("fsdp", None),
            P("tensor", None, "fsdp"),
            P("tensor", None, "fsdp"),
            P("tensor", None, "fsdp"),
            P(None, None, "fsdp", "tensor"),
            P(),
            P(),
        ),
        out_specs=(
            P("fsdp", "tensor"),
            P(None, "tensor"),
            P(None, "tensor"),
            P(None, "tensor"),
            P(None, "tensor", None, None),
        ),
        check_vma=False,
    )
```

```python
import functools
import jax
import jax.numpy as jnp
from jax import lax
from jax.experimental import pallas as pl
from jax.experimental.pallas import tpu as pltpu
from jax.sharding import PartitionSpec as P

LEN = 256
SUB = 8
MESH = pl.DeviceIdType.MESH


def recur_body(prompts, x_ref, pre_ref, g_ref, r_ref, o_ref, a_s, d_s, carry):
    @pl.when(pl.program_id(1) == 0)
    def _():
        carry[...] = jnp.zeros_like(carry)

    dims = (((1,), (1,)), ((), ()))
    x = x_ref[...]
    pre_r = lax.dot_general(x, g_ref[0, 0], dims, preferred_element_type=jnp.float32)
    pre_i = lax.dot_general(x, g_ref[1, 0], dims, preferred_element_type=jnp.float32)
    a = jnp.exp(r_ref[0] * jax.nn.sigmoid(pre_r))
    a_s[...] = a
    d_s[...] = jnp.sqrt(jnp.maximum(1.0 - a * a, 0.0)) * (
        jax.nn.sigmoid(pre_i) * x.astype(jnp.float32)
    )
    rows, chan = a_s.shape
    group = lax.broadcasted_iota(jnp.int32, (SUB, chan), 0) // prompts

    def last(v):
        res = v
        for g in range(SUB // prompts - 1):
            res = jnp.where(group == g, pltpu.roll(v, (g + 1) * prompts, 0), res)
        return res

    def step(i, c):
        at = pl.ds(pl.multiple_of(i * SUB, SUB), SUB)
        a = a_s[at, :]
        d = d_s[at, :]
        shift = 1
        while shift < SUB // prompts:
            a_sh = pltpu.roll(a, shift * prompts, 0)
            d_sh = pltpu.roll(d, shift * prompts, 0)
            d = jnp.where(group >= shift, a * d_sh + d, d)
            a = jnp.where(group >= shift, a * a_sh, a)
            shift *= 2
        d_s[at, :] = a * c + d
        return last(a) * c + last(d)

    carry[...] = lax.fori_loop(0, rows // SUB, step, carry[...], unroll=8)
    o_ref[...] = (d_s[...] * jax.nn.gelu(pre_ref[...], approximate=True)).astype(o_ref.dtype)


def recur(branch_in, gate_pre, gates, rate, prompts):
    rows, width = branch_in.shape
    blocks, chan = gates.shape[1], gates.shape[2]
    tile = min(rows, 256)
    return pl.pallas_call(
        functools.partial(recur_body, prompts),
        grid=(blocks, rows // tile),
        in_specs=[
            pl.BlockSpec((tile, chan), lambda b, t: (t, b)),
            pl.BlockSpec((tile, chan), lambda b, t: (t, b)),
            pl.BlockSpec((2, 1, chan, chan), lambda b, t: (0, b, 0, 0)),
            pl.BlockSpec((1, 1, chan), lambda b, t: (b, 0, 0)),
        ],
        out_specs=pl.BlockSpec((tile, chan), lambda b, t: (t, b)),
        out_shape=jax.ShapeDtypeStruct((rows, width), jnp.bfloat16),
        scratch_shapes=[
            pltpu.VMEM((tile, chan), jnp.float32),
            pltpu.VMEM((tile, chan), jnp.float32),
            pltpu.VMEM((SUB, chan), jnp.float32),
        ],
        compiler_params=pltpu.CompilerParams(dimension_semantics=("arbitrary", "arbitrary")),
        cost_estimate=pl.CostEstimate(
            flops=4 * rows * width * chan, bytes_accessed=8 * rows * width, transcendentals=6 * rows * width
        ),
        name="recur",
    )(branch_in, gate_pre, gates, rate)


def spread_body(g0, g1, g2, out0, out1, piece2, held, piece, own_sem, z_send, z_recv, put_sem, f_send, f_recv):
    gs, outs = (g0, g1, g2), (out0, out1)
    z, f = lax.axis_index("tensor"), lax.axis_index("fsdp")
    zs = held.shape[1]
    per = held.shape[2]
    rows = piece.shape[1]
    half = rows // 2
    sib = f + 1 - 2 * (f % 2)
    xp = f + 2 - 4 * ((f // 2) % 2)
    yp = f + 4 - 8 * (f // 4)

    barrier = pltpu.get_barrier_semaphore()
    for peer in (sib, xp, yp):
        pl.semaphore_signal(barrier, inc=1, device_id={"fsdp": peer}, device_id_type=MESH)
    for k in range(1, zs):
        pl.semaphore_signal(
            barrier, inc=1, device_id={"tensor": (z + k) % zs}, device_id_type=MESH
        )
    pl.semaphore_wait(barrier, 3 + zs - 1)

    a2a, own = {}, {}
    for w in range(3):
        for k in range(1, zs):
            to = (z + k) % zs
            a2a[w, k] = pltpu.make_async_remote_copy(
                src_ref=gs[w].at[pl.ds(to * per, per)],
                dst_ref=held.at[w, z],
                send_sem=z_send.at[w, k],
                recv_sem=z_recv.at[w, k],
                device_id={"tensor": to},
                device_id_type=MESH,
            )
            a2a[w, k].start()
        own[w] = pltpu.make_async_copy(gs[w].at[pl.ds(z * per, per)], held.at[w, z], own_sem.at[w])
        own[w].start()

    def assemble(w, dst):
        own[w].wait()
        for k in range(1, zs):
            a2a[w, k].wait_recv()
        for b in range(per):
            slab = jnp.concatenate([held[w, s, b] for s in range(zs)], axis=0)
            width = slab.shape[0]
            dst[:, b * width : (b + 1) * width] = slab.T

    sent = {}

    def send(w, i, src, start, count, peer):
        at = outs[w].at[pl.ds(start, count)]
        sent[w, i] = pltpu.make_async_remote_copy(
            src_ref=at if src is None else src,
            dst_ref=at,
            send_sem=f_send.at[w, i],
            recv_sem=f_recv.at[w, i],
            device_id={"fsdp": peer},
            device_id_type=MESH,
        )
        sent[w, i].start()

    put = {}
    diag = xp + 4 - 8 * (xp // 4)
    for w in range(2):
        assemble(w, piece.at[w])
        send(w, 0, piece.at[w], f * rows, rows, xp)
        send(w, 1, piece.at[w], f * rows, rows, yp)
        send(w, 2, piece.at[w], f * rows, rows, sib)
        put[w] = pltpu.make_async_copy(piece.at[w], outs[w].at[pl.ds(f * rows, rows)], put_sem.at[w])
        put[w].start()
    for w in range(2):
        sent[w, 0].wait_recv()
        send(w, 3, None, xp * rows, half, yp)
        send(w, 4, None, xp * rows, rows, sib)
        sent[w, 1].wait_recv()
        send(w, 5, None, yp * rows + half, half, xp)
        send(w, 6, None, yp * rows, rows, sib)
        if w == 0:
            assemble(2, piece2)
    for w in range(2):
        sent[w, 3].wait_recv()
        send(w, 7, None, diag * rows, half, sib)
        sent[w, 5].wait_recv()
        send(w, 8, None, diag * rows + half, half, sib)
    for w in range(2):
        for i in (2, 4, 6, 7, 8):
            sent[w, i].wait_recv()
        for i in range(9):
            sent[w, i].wait_send()
        put[w].wait()
    for w in range(3):
        for k in range(1, zs):
            a2a[w, k].wait_send()


def spread(groups, zs, fs):
    blocks, chan, rows = groups[0].shape
    per = blocks // zs
    width = per * chan * zs
    full = jax.ShapeDtypeStruct((rows * fs, width), jnp.bfloat16)
    vmem = pl.BlockSpec(memory_space=pltpu.VMEM)
    hbm = pl.BlockSpec(memory_space=pl.ANY)
    dma = pltpu.SemaphoreType.DMA
    return pl.pallas_call(
        spread_body,
        in_specs=[vmem] * 3,
        out_specs=[hbm, hbm, vmem],
        out_shape=[full, full, jax.ShapeDtypeStruct((rows, width), jnp.bfloat16)],
        scratch_shapes=[
            pltpu.VMEM((3, zs, per, chan, rows), jnp.bfloat16),
            pltpu.VMEM((2, rows, width), jnp.bfloat16),
            dma((3,)),
            dma((3, zs)),
            dma((3, zs)),
            dma((2,)),
            dma((2, 9)),
            dma((2, 9)),
        ],
        compiler_params=pltpu.CompilerParams(collective_id=0, has_side_effects=True),
        name="spread",
    )(*groups)


def dup_body(x_ref, o_ref):
    o_ref[...] = x_ref[...]


def dup(x):
    rows, width = x.shape
    tile = min(rows, 512)
    spec = pl.BlockSpec((tile, width), lambda i: (i, 0))
    return pl.pallas_call(
        dup_body,
        grid=(rows // tile,),
        in_specs=[spec],
        out_specs=spec,
        out_shape=jax.ShapeDtypeStruct(x.shape, x.dtype),
        cost_estimate=pl.CostEstimate(flops=0, bytes_accessed=4 * rows * width, transcendentals=0),
        name="dup",
    )(x)


def on_device(
    tokens, input_source, branch_source, output_source, gates_source, decay_param, block_order
):
    tensor_count = lax.axis_size("tensor")
    per_dev = block_order.shape[0] // tensor_count
    own_blocks = lax.dynamic_slice_in_dim(block_order, lax.axis_index("tensor") * per_dev, per_dev)
    casted = (
        input_source.astype(jnp.bfloat16),
        branch_source.astype(jnp.bfloat16),
        output_source.astype(jnp.bfloat16),
    )
    gate_cast = gates_source.astype(jnp.bfloat16)
    sectioned = tuple((jnp.take(weight, block_order, axis=1) for weight in casted))
    gate_sectioned = jnp.take(gate_cast, block_order, axis=1)
    gate_group = lax.all_to_all(gate_sectioned, "tensor", split_axis=1, concat_axis=3, tiled=True)
    gate_piece = jnp.transpose(gate_group, (0, 1, 3, 2))
    gates_serve = lax.all_gather(gate_piece, "fsdp", axis=3, tiled=True)
    row_count = tokens.shape[0]
    if lax.axis_size("fsdp") == 8:
        groups = [jnp.transpose(weight, (1, 0, 2)) for weight in sectioned]
        input_serve, branch_serve, output_piece = spread(groups, tensor_count, 8)
    else:
        regrouped = lax.all_to_all(sectioned, "tensor", split_axis=1, concat_axis=0, tiled=True)
        pieces = tuple(
            (jnp.transpose(weight, (2, 1, 0)).reshape(weight.shape[2], -1) for weight in regrouped)
        )
        input_serve = lax.all_gather(pieces[0], "fsdp", axis=0, tiled=True)
        branch_serve = lax.all_gather(pieces[1], "fsdp", axis=0, tiled=True)
        output_piece = pieces[2]
    output_serve = lax.all_gather(output_piece, "fsdp", axis=0, tiled=True)
    rate = -8.0 * jax.nn.softplus(jnp.take(decay_param, own_blocks, axis=0))[:, None, :]
    branch_in = jnp.dot(tokens, input_serve, preferred_element_type=jnp.float32).astype(jnp.bfloat16)
    gate_pre = jnp.dot(tokens, branch_serve, preferred_element_type=jnp.float32)
    gated = recur(branch_in, gate_pre, gates_serve, rate, row_count // LEN)
    parts = []
    for rows in jnp.split(gated, 2, axis=0):
        partial_value = lax.dot_general(
            rows, output_serve, (((1,), (1,)), ((), ())), preferred_element_type=jnp.float32
        )
        parts.append(
            lax.psum_scatter(
                partial_value.astype(jnp.bfloat16), "tensor", scatter_dimension=1, tiled=True
            )
        )
    mixed = jnp.concatenate(parts, axis=0)
    return (mixed, dup(input_serve), dup(branch_serve), dup(output_serve), gates_serve)


def solution(mesh):
    return jax.shard_map(
        on_device,
        mesh=mesh,
        in_specs=(
            P("fsdp", None),
            P("tensor", None, "fsdp"),
            P("tensor", None, "fsdp"),
            P("tensor", None, "fsdp"),
            P(None, None, "fsdp", "tensor"),
            P(),
            P(),
        ),
        out_specs=(
            P("fsdp", "tensor"),
            P(None, "tensor"),
            P(None, "tensor"),
            P(None, "tensor"),
            P(None, "tensor", None, None),
        ),
        check_vma=False,
    )
```

```python
import functools
import jax
import jax.numpy as jnp
from jax import lax
from jax.experimental import pallas as pl
from jax.experimental.pallas import tpu as pltpu
from jax.sharding import PartitionSpec as P

LEN = 256
SUB = 8
MESH = pl.DeviceIdType.MESH


def recur_body(prompts, x_ref, pre_ref, g_ref, r_ref, o_ref, a_s, d_s, carry):
    @pl.when(pl.program_id(1) == 0)
    def _():
        carry[...] = jnp.zeros_like(carry)

    dims = (((1,), (1,)), ((), ()))
    x = x_ref[...]
    pre_r = lax.dot_general(x, g_ref[0, 0], dims, preferred_element_type=jnp.float32)
    pre_i = lax.dot_general(x, g_ref[1, 0], dims, preferred_element_type=jnp.float32)
    a = jnp.exp(r_ref[0] * jax.nn.sigmoid(pre_r))
    a_s[...] = a
    d_s[...] = jnp.sqrt(jnp.maximum(1.0 - a * a, 0.0)) * (
        jax.nn.sigmoid(pre_i) * x.astype(jnp.float32)
    )
    rows, chan = a_s.shape
    group = lax.broadcasted_iota(jnp.int32, (SUB, chan), 0) // prompts

    def last(v):
        res = v
        for g in range(SUB // prompts - 1):
            res = jnp.where(group == g, pltpu.roll(v, (g + 1) * prompts, 0), res)
        return res

    def step(i, c):
        at = pl.ds(pl.multiple_of(i * SUB, SUB), SUB)
        a = a_s[at, :]
        d = d_s[at, :]
        shift = 1
        while shift < SUB // prompts:
            a_sh = pltpu.roll(a, shift * prompts, 0)
            d_sh = pltpu.roll(d, shift * prompts, 0)
            d = jnp.where(group >= shift, a * d_sh + d, d)
            a = jnp.where(group >= shift, a * a_sh, a)
            shift *= 2
        d_s[at, :] = a * c + d
        return last(a) * c + last(d)

    carry[...] = lax.fori_loop(0, rows // SUB, step, carry[...], unroll=8)
    o_ref[...] = (d_s[...] * jax.nn.gelu(pre_ref[...], approximate=True)).astype(o_ref.dtype)


def recur(branch_in, gate_pre, gates, rate, prompts):
    rows, width = branch_in.shape
    blocks, chan = gates.shape[1], gates.shape[2]
    tile = min(rows, 256)
    return pl.pallas_call(
        functools.partial(recur_body, prompts),
        grid=(blocks, rows // tile),
        in_specs=[
            pl.BlockSpec((tile, chan), lambda b, t: (t, b)),
            pl.BlockSpec((tile, chan), lambda b, t: (t, b)),
            pl.BlockSpec((2, 1, chan, chan), lambda b, t: (0, b, 0, 0)),
            pl.BlockSpec((1, 1, chan), lambda b, t: (b, 0, 0)),
        ],
        out_specs=pl.BlockSpec((tile, chan), lambda b, t: (t, b)),
        out_shape=jax.ShapeDtypeStruct((rows, width), jnp.bfloat16),
        scratch_shapes=[
            pltpu.VMEM((tile, chan), jnp.float32),
            pltpu.VMEM((tile, chan), jnp.float32),
            pltpu.VMEM((SUB, chan), jnp.float32),
        ],
        compiler_params=pltpu.CompilerParams(dimension_semantics=("arbitrary", "arbitrary")),
        cost_estimate=pl.CostEstimate(
            flops=4 * rows * width * chan, bytes_accessed=8 * rows * width, transcendentals=6 * rows * width
        ),
        name="recur",
    )(branch_in, gate_pre, gates, rate)


def spread_body(
    g0, g1, g2, gg, out0, out1, piece2, gates_out,
    held, piece, gheld, gpiece, gfull, own_sem, z_send, z_recv, put_sem, f_send, f_recv,
):
    gs = (g0, g1, g2)
    z, f = lax.axis_index("tensor"), lax.axis_index("fsdp")
    zs, per = held.shape[1], held.shape[2]
    half = piece.shape[1]
    rows = 2 * half
    ghalf = gpiece.shape[3]
    sib = f + 1 - 2 * (f % 2)
    xp = f + 2 - 4 * ((f // 2) % 2)
    yp = f + 4 - 8 * (f // 4)
    diag = xp + 4 - 8 * (xp // 4)

    barrier = pltpu.get_barrier_semaphore()
    for peer in (sib, xp, yp):
        pl.semaphore_signal(barrier, inc=1, device_id={"fsdp": peer}, device_id_type=MESH)
    for k in range(1, zs):
        pl.semaphore_signal(
            barrier, inc=1, device_id={"tensor": (z + k) % zs}, device_id_type=MESH
        )
    pl.semaphore_wait(barrier, 3 + zs - 1)

    def z_source(q, to):
        if q == 6:
            return gg.at[:, pl.ds(to * per, per)]
        return gs[q // 2].at[pl.ds(to * per, per), :, pl.ds((q % 2) * half, half)]

    def z_target(q):
        if q == 6:
            return gheld.at[z]
        return held.at[q // 2, z, :, :, pl.ds((q % 2) * half, half)]

    a2a, own = {}, {}
    for q in (0, 1, 2, 6, 3, 4, 5):
        for k in range(1, zs):
            to = (z + k) % zs
            a2a[q, k] = pltpu.make_async_remote_copy(
                src_ref=z_source(q, to),
                dst_ref=z_target(q),
                send_sem=z_send.at[q, k],
                recv_sem=z_recv.at[q, k],
                device_id={"tensor": to},
                device_id_type=MESH,
            )
            a2a[q, k].start()
        own[q] = pltpu.make_async_copy(z_source(q, z), z_target(q), own_sem.at[q])
        own[q].start()

    def arrive(q):
        own[q].wait()
        for k in range(1, zs):
            a2a[q, k].wait_recv()

    def assemble(q, dst):
        arrive(q)
        at = slice((q % 2) * half, (q % 2) * half + half)
        for b in range(per):
            slab = jnp.concatenate([held[q // 2, s, b, :, at] for s in range(zs)], axis=0)
            width = slab.shape[0]
            dst[:, b * width : (b + 1) * width] = slab.T

    def view(q, owner):
        if q >= 4:
            return gfull.at[:, :, pl.ds(owner * 2 * ghalf + (q - 4) * ghalf, ghalf)]
        return (out0, out1)[q // 2].at[pl.ds(owner * rows + (q % 2) * half, half)]

    sent, put = {}, {}

    def send(q, i, src, owner, peer):
        at = view(q, owner)
        sent[q, i] = pltpu.make_async_remote_copy(
            src_ref=at if src is None else src,
            dst_ref=at,
            send_sem=f_send.at[q, i],
            recv_sem=f_recv.at[q, i],
            device_id={"fsdp": peer},
            device_id_type=MESH,
        )
        sent[q, i].start()

    def first(q):
        if q >= 4:
            src = gpiece.at[q - 4]
        else:
            src = piece.at[q]
            assemble(q, src)
        for i, peer in enumerate((xp, yp, sib)):
            send(q, i, src, f, peer)
        put[q] = pltpu.make_async_copy(src, view(q, f), put_sem.at[q])
        put[q].start()

    def relay(q):
        sent[q, 0].wait_recv()
        if q % 2 == 0:
            send(q, 3, None, xp, yp)
        send(q, 4, None, xp, sib)
        sent[q, 1].wait_recv()
        if q % 2 == 1:
            send(q, 3, None, yp, xp)
        send(q, 5, None, yp, sib)

    def across(q):
        sent[q, 3].wait_recv()
        send(q, 6, None, diag, sib)

    first(0)
    first(1)
    relay(0)
    first(2)
    arrive(6)
    for h in range(2):
        for g in range(gpiece.shape[1]):
            for b in range(per):
                gpiece[h, g, b] = jnp.concatenate(
                    [gheld[s, g, b, h * ghalf : (h + 1) * ghalf, :] for s in range(zs)], axis=1
                )
    first(4)
    first(5)
    relay(1)
    first(3)
    across(0)
    relay(2)
    relay(4)
    relay(5)
    assemble(4, piece2.at[pl.ds(0, half)])
    across(1)
    relay(3)
    assemble(5, piece2.at[pl.ds(half, half)])
    for q in (4, 5, 2, 3):
        across(q)
    for q in (4, 5):
        for i in (2, 4, 5, 6):
            sent[q, i].wait_recv()
        put[q].wait()
    for g in range(gfull.shape[0]):
        for b in range(per):
            gates_out[g, b] = gfull[g, b].T
    for q in range(4):
        for i in (2, 4, 5, 6):
            sent[q, i].wait_recv()
        put[q].wait()
    for q in range(6):
        for i in range(7):
            sent[q, i].wait_send()
    for q in range(7):
        for k in range(1, zs):
            a2a[q, k].wait_send()


def spread(groups, gates, zs, fs):
    blocks, chan, rows = groups[0].shape
    kinds, _, gin, gout = gates.shape
    per = blocks // zs
    width = per * chan * zs
    full = jax.ShapeDtypeStruct((rows * fs, width), jnp.bfloat16)
    square = (kinds, per, gin * fs, gout * zs)
    vmem = pl.BlockSpec(memory_space=pltpu.VMEM)
    hbm = pl.BlockSpec(memory_space=pl.ANY)
    dma = pltpu.SemaphoreType.DMA
    return pl.pallas_call(
        spread_body,
        in_specs=[vmem] * 4,
        out_specs=[hbm, hbm, vmem, vmem],
        out_shape=[
            full,
            full,
            jax.ShapeDtypeStruct((rows, width), jnp.bfloat16),
            jax.ShapeDtypeStruct((kinds, per, gout * zs, gin * fs), jnp.bfloat16),
        ],
        scratch_shapes=[
            pltpu.VMEM((3, zs, per, chan, rows), jnp.bfloat16),
            pltpu.VMEM((4, rows // 2, width), jnp.bfloat16),
            pltpu.VMEM((zs, kinds, per, gin, gout), jnp.bfloat16),
            pltpu.VMEM((2, kinds, per, gin // 2, gout * zs), jnp.bfloat16),
            pltpu.VMEM(square, jnp.bfloat16),
            dma((7,)),
            dma((7, zs)),
            dma((7, zs)),
            dma((6,)),
            dma((6, 7)),
            dma((6, 7)),
        ],
        compiler_params=pltpu.CompilerParams(collective_id=0, has_side_effects=True),
        name="spread",
    )(*groups, gates)


def dup_body(x_ref, o_ref):
    o_ref[...] = x_ref[...]


def dup(x):
    rows, width = x.shape
    tile = min(rows, 512)
    spec = pl.BlockSpec((tile, width), lambda i: (i, 0))
    return pl.pallas_call(
        dup_body,
        grid=(rows // tile,),
        in_specs=[spec],
        out_specs=spec,
        out_shape=jax.ShapeDtypeStruct(x.shape, x.dtype),
        cost_estimate=pl.CostEstimate(flops=0, bytes_accessed=4 * rows * width, transcendentals=0),
        name="dup",
    )(x)


def on_device(
    tokens, input_source, branch_source, output_source, gates_source, decay_param, block_order
):
    tensor_count = lax.axis_size("tensor")
    per_dev = block_order.shape[0] // tensor_count
    own_blocks = lax.dynamic_slice_in_dim(block_order, lax.axis_index("tensor") * per_dev, per_dev)
    casted = (
        input_source.astype(jnp.bfloat16),
        branch_source.astype(jnp.bfloat16),
        output_source.astype(jnp.bfloat16),
    )
    gate_cast = gates_source.astype(jnp.bfloat16)
    sectioned = tuple((jnp.take(weight, block_order, axis=1) for weight in casted))
    gate_sectioned = jnp.take(gate_cast, block_order, axis=1)
    row_count = tokens.shape[0]
    if lax.axis_size("fsdp") == 8:
        groups = [jnp.transpose(weight, (1, 0, 2)) for weight in sectioned]
        input_serve, branch_serve, output_piece, gates_serve = spread(
            groups, gate_sectioned, tensor_count, 8
        )
    else:
        gate_group = lax.all_to_all(gate_sectioned, "tensor", split_axis=1, concat_axis=3, tiled=True)
        gate_piece = jnp.transpose(gate_group, (0, 1, 3, 2))
        gates_serve = lax.all_gather(gate_piece, "fsdp", axis=3, tiled=True)
        regrouped = lax.all_to_all(sectioned, "tensor", split_axis=1, concat_axis=0, tiled=True)
        pieces = tuple(
            (jnp.transpose(weight, (2, 1, 0)).reshape(weight.shape[2], -1) for weight in regrouped)
        )
        input_serve = lax.all_gather(pieces[0], "fsdp", axis=0, tiled=True)
        branch_serve = lax.all_gather(pieces[1], "fsdp", axis=0, tiled=True)
        output_piece = pieces[2]
    output_serve = lax.all_gather(output_piece, "fsdp", axis=0, tiled=True)
    rate = -8.0 * jax.nn.softplus(jnp.take(decay_param, own_blocks, axis=0))[:, None, :]
    branch_in = jnp.dot(tokens, input_serve, preferred_element_type=jnp.float32).astype(jnp.bfloat16)
    gate_pre = jnp.dot(tokens, branch_serve, preferred_element_type=jnp.float32)
    gated = recur(branch_in, gate_pre, gates_serve, rate, row_count // LEN)
    parts = []
    for rows in jnp.split(gated, [row_count // 8], axis=0):
        partial_value = lax.dot_general(
            rows, output_serve, (((1,), (1,)), ((), ())), preferred_element_type=jnp.float32
        )
        parts.append(
            lax.psum_scatter(
                partial_value.astype(jnp.bfloat16), "tensor", scatter_dimension=1, tiled=True
            )
        )
    mixed = jnp.concatenate(parts, axis=0)
    return (mixed, dup(input_serve), dup(branch_serve), dup(output_serve), gates_serve)


def solution(mesh):
    return jax.shard_map(
        on_device,
        mesh=mesh,
        in_specs=(
            P("fsdp", None),
            P("tensor", None, "fsdp"),
            P("tensor", None, "fsdp"),
            P("tensor", None, "fsdp"),
            P(None, None, "fsdp", "tensor"),
            P(),
            P(),
        ),
        out_specs=(
            P("fsdp", "tensor"),
            P(None, "tensor"),
            P(None, "tensor"),
            P(None, "tensor"),
            P(None, "tensor", None, None),
        ),
        check_vma=False,
    )
```

```python
import functools
import jax
import jax.numpy as jnp
from jax import lax
from jax.experimental import pallas as pl
from jax.experimental.pallas import tpu as pltpu
from jax.sharding import PartitionSpec as P

LEN = 256
SUB = 8
MESH = pl.DeviceIdType.MESH


def recur_body(prompts, x_ref, pre_ref, g_ref, r_ref, o_ref, a_s, d_s, carry):
    @pl.when(pl.program_id(1) == 0)
    def _():
        carry[...] = jnp.zeros_like(carry)

    dims = (((1,), (1,)), ((), ()))
    x = x_ref[...]
    pre_r = lax.dot_general(x, g_ref[0, 0], dims, preferred_element_type=jnp.float32)
    pre_i = lax.dot_general(x, g_ref[1, 0], dims, preferred_element_type=jnp.float32)
    a = jnp.exp(r_ref[0] * jax.nn.sigmoid(pre_r))
    a_s[...] = a
    d_s[...] = jnp.sqrt(jnp.maximum(1.0 - a * a, 0.0)) * (
        jax.nn.sigmoid(pre_i) * x.astype(jnp.float32)
    )
    rows, chan = a_s.shape
    group = lax.broadcasted_iota(jnp.int32, (SUB, chan), 0) // prompts

    def last(v):
        res = v
        for g in range(SUB // prompts - 1):
            res = jnp.where(group == g, pltpu.roll(v, (g + 1) * prompts, 0), res)
        return res

    def step(i, c):
        at = pl.ds(pl.multiple_of(i * SUB, SUB), SUB)
        a = a_s[at, :]
        d = d_s[at, :]
        shift = 1
        while shift < SUB // prompts:
            a_sh = pltpu.roll(a, shift * prompts, 0)
            d_sh = pltpu.roll(d, shift * prompts, 0)
            d = jnp.where(group >= shift, a * d_sh + d, d)
            a = jnp.where(group >= shift, a * a_sh, a)
            shift *= 2
        d_s[at, :] = a * c + d
        return last(a) * c + last(d)

    carry[...] = lax.fori_loop(0, rows // SUB, step, carry[...], unroll=8)
    o_ref[...] = (d_s[...] * jax.nn.gelu(pre_ref[...], approximate=True)).astype(o_ref.dtype)


def recur(branch_in, gate_pre, gates, rate, prompts):
    rows, width = branch_in.shape
    blocks, chan = gates.shape[1], gates.shape[2]
    tile = min(rows, 256)
    return pl.pallas_call(
        functools.partial(recur_body, prompts),
        grid=(blocks, rows // tile),
        in_specs=[
            pl.BlockSpec((tile, chan), lambda b, t: (t, b)),
            pl.BlockSpec((tile, chan), lambda b, t: (t, b)),
            pl.BlockSpec((2, 1, chan, chan), lambda b, t: (0, b, 0, 0)),
            pl.BlockSpec((1, 1, chan), lambda b, t: (b, 0, 0)),
        ],
        out_specs=pl.BlockSpec((tile, chan), lambda b, t: (t, b)),
        out_shape=jax.ShapeDtypeStruct((rows, width), jnp.bfloat16),
        scratch_shapes=[
            pltpu.VMEM((tile, chan), jnp.float32),
            pltpu.VMEM((tile, chan), jnp.float32),
            pltpu.VMEM((SUB, chan), jnp.float32),
        ],
        compiler_params=pltpu.CompilerParams(dimension_semantics=("arbitrary", "arbitrary")),
        cost_estimate=pl.CostEstimate(
            flops=4 * rows * width * chan, bytes_accessed=8 * rows * width, transcendentals=6 * rows * width
        ),
        name="recur",
    )(branch_in, gate_pre, gates, rate)


def spread_body(
    g0, g1, g2, gg, out0, out1, piece2, gates_out,
    held, piece, gheld, gpiece, gfull, own_sem, z_send, z_recv, put_sem, f_send, f_recv,
):
    gs = (g0, g1, g2)
    z, f = lax.axis_index("tensor"), lax.axis_index("fsdp")
    zs, per = held.shape[1], held.shape[2]
    half = piece.shape[1]
    rows = 2 * half
    ghalf = gpiece.shape[3]
    sib = f + 1 - 2 * (f % 2)
    xp = f + 2 - 4 * ((f // 2) % 2)
    yp = f + 4 - 8 * (f // 4)
    diag = xp + 4 - 8 * (xp // 4)

    barrier = pltpu.get_barrier_semaphore()
    for peer in (sib, xp, yp):
        pl.semaphore_signal(barrier, inc=1, device_id={"fsdp": peer}, device_id_type=MESH)
    for k in range(1, zs):
        pl.semaphore_signal(
            barrier, inc=1, device_id={"tensor": (z + k) % zs}, device_id_type=MESH
        )
    pl.semaphore_wait(barrier, 3 + zs - 1)

    def z_source(q, to):
        if q == 6:
            return gg.at[:, pl.ds(to * per, per)]
        return gs[q // 2].at[pl.ds(to * per, per), :, pl.ds((q % 2) * half, half)]

    def z_target(q):
        if q == 6:
            return gheld.at[z]
        return held.at[q // 2, z, :, :, pl.ds((q % 2) * half, half)]

    a2a, own = {}, {}
    queue = [0, 1, 2, 6, 3, 4, 5]

    def depart():
        q = queue.pop(0)
        for k in range(1, zs):
            to = (z + k) % zs
            a2a[q, k] = pltpu.make_async_remote_copy(
                src_ref=z_source(q, to),
                dst_ref=z_target(q),
                send_sem=z_send.at[q, k],
                recv_sem=z_recv.at[q, k],
                device_id={"tensor": to},
                device_id_type=MESH,
            )
            a2a[q, k].start()
        own[q] = pltpu.make_async_copy(z_source(q, z), z_target(q), own_sem.at[q])
        own[q].start()

    depart()
    depart()

    def arrive(q):
        own[q].wait()
        for k in range(1, zs):
            a2a[q, k].wait_recv()
        if queue:
            depart()

    def assemble(q, dst):
        arrive(q)
        at = slice((q % 2) * half, (q % 2) * half + half)
        for b in range(per):
            slab = jnp.concatenate([held[q // 2, s, b, :, at] for s in range(zs)], axis=0)
            width = slab.shape[0]
            dst[:, b * width : (b + 1) * width] = slab.T

    def view(q, owner):
        if q >= 4:
            return gfull.at[:, :, pl.ds(owner * 2 * ghalf + (q - 4) * ghalf, ghalf)]
        return (out0, out1)[q // 2].at[pl.ds(owner * rows + (q % 2) * half, half)]

    sent, put = {}, {}

    def send(q, i, src, owner, peer):
        at = view(q, owner)
        sent[q, i] = pltpu.make_async_remote_copy(
            src_ref=at if src is None else src,
            dst_ref=at,
            send_sem=f_send.at[q, i],
            recv_sem=f_recv.at[q, i],
            device_id={"fsdp": peer},
            device_id_type=MESH,
        )
        sent[q, i].start()

    def first(q):
        if q >= 4:
            src = gpiece.at[q - 4]
        else:
            src = piece.at[q]
            assemble(q, src)
        for i, peer in enumerate((xp, yp, sib)):
            send(q, i, src, f, peer)
        put[q] = pltpu.make_async_copy(src, view(q, f), put_sem.at[q])
        put[q].start()

    def relay(q):
        sent[q, 0].wait_recv()
        if q % 2 == 0:
            send(q, 3, None, xp, yp)
        send(q, 4, None, xp, sib)
        sent[q, 1].wait_recv()
        if q % 2 == 1:
            send(q, 3, None, yp, xp)
        send(q, 5, None, yp, sib)

    def across(q):
        sent[q, 3].wait_recv()
        send(q, 6, None, diag, sib)

    first(0)
    first(1)
    relay(0)
    first(2)
    arrive(6)
    for h in range(2):
        for g in range(gpiece.shape[1]):
            for b in range(per):
                gpiece[h, g, b] = jnp.concatenate(
                    [gheld[s, g, b, h * ghalf : (h + 1) * ghalf, :] for s in range(zs)], axis=1
                )
    first(4)
    first(5)
    relay(1)
    first(3)
    across(0)
    relay(2)
    relay(4)
    relay(5)
    assemble(4, piece2.at[pl.ds(0, half)])
    across(1)
    relay(3)
    assemble(5, piece2.at[pl.ds(half, half)])
    for q in (4, 5, 2, 3):
        across(q)
    for q in (4, 5):
        for i in (2, 4, 5, 6):
            sent[q, i].wait_recv()
        put[q].wait()
    for g in range(gfull.shape[0]):
        for b in range(per):
            gates_out[g, b] = gfull[g, b].T
    for q in range(4):
        for i in (2, 4, 5, 6):
            sent[q, i].wait_recv()
        put[q].wait()
    for q in range(6):
        for i in range(7):
            sent[q, i].wait_send()
    for q in range(7):
        for k in range(1, zs):
            a2a[q, k].wait_send()


def spread(groups, gates, zs, fs):
    blocks, chan, rows = groups[0].shape
    kinds, _, gin, gout = gates.shape
    per = blocks // zs
    width = per * chan * zs
    full = jax.ShapeDtypeStruct((rows * fs, width), jnp.bfloat16)
    square = (kinds, per, gin * fs, gout * zs)
    vmem = pl.BlockSpec(memory_space=pltpu.VMEM)
    hbm = pl.BlockSpec(memory_space=pl.ANY)
    dma = pltpu.SemaphoreType.DMA
    return pl.pallas_call(
        spread_body,
        in_specs=[vmem] * 4,
        out_specs=[hbm, hbm, vmem, vmem],
        out_shape=[
            full,
            full,
            jax.ShapeDtypeStruct((rows, width), jnp.bfloat16),
            jax.ShapeDtypeStruct((kinds, per, gout * zs, gin * fs), jnp.bfloat16),
        ],
        scratch_shapes=[
            pltpu.VMEM((3, zs, per, chan, rows), jnp.bfloat16),
            pltpu.VMEM((4, rows // 2, width), jnp.bfloat16),
            pltpu.VMEM((zs, kinds, per, gin, gout), jnp.bfloat16),
            pltpu.VMEM((2, kinds, per, gin // 2, gout * zs), jnp.bfloat16),
            pltpu.VMEM(square, jnp.bfloat16),
            dma((7,)),
            dma((7, zs)),
            dma((7, zs)),
            dma((6,)),
            dma((6, 7)),
            dma((6, 7)),
        ],
        compiler_params=pltpu.CompilerParams(collective_id=0, has_side_effects=True),
        name="spread",
    )(*groups, gates)


def dup_body(x_ref, o_ref):
    o_ref[...] = x_ref[...]


def dup(x):
    rows, width = x.shape
    tile = min(rows, 512)
    spec = pl.BlockSpec((tile, width), lambda i: (i, 0))
    return pl.pallas_call(
        dup_body,
        grid=(rows // tile,),
        in_specs=[spec],
        out_specs=spec,
        out_shape=jax.ShapeDtypeStruct(x.shape, x.dtype),
        cost_estimate=pl.CostEstimate(flops=0, bytes_accessed=4 * rows * width, transcendentals=0),
        name="dup",
    )(x)


def on_device(
    tokens, input_source, branch_source, output_source, gates_source, decay_param, block_order
):
    tensor_count = lax.axis_size("tensor")
    per_dev = block_order.shape[0] // tensor_count
    own_blocks = lax.dynamic_slice_in_dim(block_order, lax.axis_index("tensor") * per_dev, per_dev)
    casted = (
        input_source.astype(jnp.bfloat16),
        branch_source.astype(jnp.bfloat16),
        output_source.astype(jnp.bfloat16),
    )
    gate_cast = gates_source.astype(jnp.bfloat16)
    sectioned = tuple((jnp.take(weight, block_order, axis=1, mode="clip") for weight in casted))
    gate_sectioned = jnp.take(gate_cast, block_order, axis=1, mode="clip")
    row_count = tokens.shape[0]
    if lax.axis_size("fsdp") == 8:
        groups = [jnp.transpose(weight, (1, 0, 2)) for weight in sectioned]
        input_serve, branch_serve, output_piece, gates_serve = spread(
            groups, gate_sectioned, tensor_count, 8
        )
    else:
        gate_group = lax.all_to_all(gate_sectioned, "tensor", split_axis=1, concat_axis=3, tiled=True)
        gate_piece = jnp.transpose(gate_group, (0, 1, 3, 2))
        gates_serve = lax.all_gather(gate_piece, "fsdp", axis=3, tiled=True)
        regrouped = lax.all_to_all(sectioned, "tensor", split_axis=1, concat_axis=0, tiled=True)
        pieces = tuple(
            (jnp.transpose(weight, (2, 1, 0)).reshape(weight.shape[2], -1) for weight in regrouped)
        )
        input_serve = lax.all_gather(pieces[0], "fsdp", axis=0, tiled=True)
        branch_serve = lax.all_gather(pieces[1], "fsdp", axis=0, tiled=True)
        output_piece = pieces[2]
    output_serve = lax.all_gather(output_piece, "fsdp", axis=0, tiled=True)
    rate = -8.0 * jax.nn.softplus(jnp.take(decay_param, own_blocks, axis=0, mode="clip"))[:, None, :]
    branch_in = jnp.dot(tokens, input_serve, preferred_element_type=jnp.float32).astype(jnp.bfloat16)
    gate_pre = jnp.dot(tokens, branch_serve, preferred_element_type=jnp.float32)
    gated = recur(branch_in, gate_pre, gates_serve, rate, row_count // LEN)
    partial_value = lax.dot_general(
        gated, output_serve, (((1,), (1,)), ((), ())), preferred_element_type=jnp.float32
    )
    mixed = lax.psum_scatter(
        partial_value.astype(jnp.bfloat16), "tensor", scatter_dimension=1, tiled=True
    )
    return (mixed, dup(input_serve), dup(branch_serve), dup(output_serve), gates_serve)


def solution(mesh):
    return jax.shard_map(
        on_device,
        mesh=mesh,
        in_specs=(
            P("fsdp", None),
            P("tensor", None, "fsdp"),
            P("tensor", None, "fsdp"),
            P("tensor", None, "fsdp"),
            P(None, None, "fsdp", "tensor"),
            P(),
            P(),
        ),
        out_specs=(
            P("fsdp", "tensor"),
            P(None, "tensor"),
            P(None, "tensor"),
            P(None, "tensor"),
            P(None, "tensor", None, None),
        ),
        check_vma=False,
    )
```

```python
import functools
import jax
import jax.numpy as jnp
from jax import lax
from jax.experimental import pallas as pl
from jax.experimental.pallas import tpu as pltpu
from jax.sharding import PartitionSpec as P

LEN = 256
SUB = 8
MESH = pl.DeviceIdType.MESH


def recur_body(prompts, x_ref, pre_ref, g_ref, r_ref, o_ref, a_s, d_s, carry):
    @pl.when(pl.program_id(1) == 0)
    def _():
        carry[...] = jnp.zeros_like(carry)

    dims = (((1,), (1,)), ((), ()))
    x = x_ref[...]
    pre_r = lax.dot_general(x, g_ref[0, 0], dims, preferred_element_type=jnp.float32)
    pre_i = lax.dot_general(x, g_ref[1, 0], dims, preferred_element_type=jnp.float32)
    a = jnp.exp(r_ref[0] * jax.nn.sigmoid(pre_r))
    a_s[...] = a
    d_s[...] = jnp.sqrt(jnp.maximum(1.0 - a * a, 0.0)) * (
        jax.nn.sigmoid(pre_i) * x.astype(jnp.float32)
    )
    rows, chan = a_s.shape
    group = lax.broadcasted_iota(jnp.int32, (SUB, chan), 0) // prompts

    def last(v):
        res = v
        for g in range(SUB // prompts - 1):
            res = jnp.where(group == g, pltpu.roll(v, (g + 1) * prompts, 0), res)
        return res

    def step(i, c):
        at = pl.ds(pl.multiple_of(i * SUB, SUB), SUB)
        a = a_s[at, :]
        d = d_s[at, :]
        shift = 1
        while shift < SUB // prompts:
            a_sh = pltpu.roll(a, shift * prompts, 0)
            d_sh = pltpu.roll(d, shift * prompts, 0)
            d = jnp.where(group >= shift, a * d_sh + d, d)
            a = jnp.where(group >= shift, a * a_sh, a)
            shift *= 2
        d_s[at, :] = a * c + d
        return last(a) * c + last(d)

    carry[...] = lax.fori_loop(0, rows // SUB, step, carry[...], unroll=8)
    o_ref[...] = (d_s[...] * jax.nn.gelu(pre_ref[...], approximate=True)).astype(o_ref.dtype)


def recur(branch_in, gate_pre, gates, rate, prompts):
    rows, width = branch_in.shape
    blocks, chan = gates.shape[1], gates.shape[2]
    tile = min(rows, 256)
    return pl.pallas_call(
        functools.partial(recur_body, prompts),
        grid=(blocks, rows // tile),
        in_specs=[
            pl.BlockSpec((tile, chan), lambda b, t: (t, b)),
            pl.BlockSpec((tile, chan), lambda b, t: (t, b)),
            pl.BlockSpec((2, 1, chan, chan), lambda b, t: (0, b, 0, 0)),
            pl.BlockSpec((1, 1, chan), lambda b, t: (b, 0, 0)),
        ],
        out_specs=pl.BlockSpec((tile, chan), lambda b, t: (t, b)),
        out_shape=jax.ShapeDtypeStruct((rows, width), jnp.bfloat16),
        scratch_shapes=[
            pltpu.VMEM((tile, chan), jnp.float32),
            pltpu.VMEM((tile, chan), jnp.float32),
            pltpu.VMEM((SUB, chan), jnp.float32),
        ],
        compiler_params=pltpu.CompilerParams(dimension_semantics=("arbitrary", "arbitrary")),
        cost_estimate=pl.CostEstimate(
            flops=4 * rows * width * chan, bytes_accessed=8 * rows * width, transcendentals=6 * rows * width
        ),
        name="recur",
    )(branch_in, gate_pre, gates, rate)


def spread_body(
    g0, g1, g2, gg, out0, out1, piece2, gates_out,
    held, piece, gheld, gpiece, gfull, own_sem, z_send, z_recv, put_sem, f_send, f_recv,
):
    gs = (g0, g1, g2)
    z, f = lax.axis_index("tensor"), lax.axis_index("fsdp")
    zs, per = held.shape[1], held.shape[2]
    half = piece.shape[1]
    rows = 2 * half
    ghalf = gpiece.shape[3]
    sib = f + 1 - 2 * (f % 2)
    xp = f + 2 - 4 * ((f // 2) % 2)
    yp = f + 4 - 8 * (f // 4)
    diag = xp + 4 - 8 * (xp // 4)

    barrier = pltpu.get_barrier_semaphore()
    for peer in (sib, xp, yp):
        pl.semaphore_signal(barrier, inc=1, device_id={"fsdp": peer}, device_id_type=MESH)
    for k in range(1, zs):
        pl.semaphore_signal(
            barrier, inc=1, device_id={"tensor": (z + k) % zs}, device_id_type=MESH
        )
    pl.semaphore_wait(barrier, 3 + zs - 1)

    def z_source(q, to):
        if q == 6:
            return gg.at[:, pl.ds(to * per, per)]
        return gs[q // 2].at[pl.ds(to * per, per), :, pl.ds((q % 2) * half, half)]

    def z_target(q):
        if q == 6:
            return gheld.at[z]
        return held.at[q // 2, z, :, :, pl.ds((q % 2) * half, half)]

    a2a, own = {}, {}
    queue = [0, 1, 2, 3, 6, 4, 5]

    def depart():
        q = queue.pop(0)
        for k in range(1, zs):
            to = (z + k) % zs
            a2a[q, k] = pltpu.make_async_remote_copy(
                src_ref=z_source(q, to),
                dst_ref=z_target(q),
                send_sem=z_send.at[q, k],
                recv_sem=z_recv.at[q, k],
                device_id={"tensor": to},
                device_id_type=MESH,
            )
            a2a[q, k].start()
        own[q] = pltpu.make_async_copy(z_source(q, z), z_target(q), own_sem.at[q])
        own[q].start()

    depart()
    depart()

    def arrive(q):
        own[q].wait()
        for k in range(1, zs):
            a2a[q, k].wait_recv()
        if queue:
            depart()

    def assemble(q, dst):
        arrive(q)
        at = slice((q % 2) * half, (q % 2) * half + half)
        for b in range(per):
            slab = jnp.concatenate([held[q // 2, s, b, :, at] for s in range(zs)], axis=0)
            width = slab.shape[0]
            dst[:, b * width : (b + 1) * width] = slab.T

    def view(q, owner):
        if q >= 4:
            return gfull.at[:, :, pl.ds(owner * 2 * ghalf + (q - 4) * ghalf, ghalf)]
        return (out0, out1)[q // 2].at[pl.ds(owner * rows + (q % 2) * half, half)]

    sent, put = {}, {}

    def send(q, i, src, owner, peer):
        at = view(q, owner)
        sent[q, i] = pltpu.make_async_remote_copy(
            src_ref=at if src is None else src,
            dst_ref=at,
            send_sem=f_send.at[q, i],
            recv_sem=f_recv.at[q, i],
            device_id={"fsdp": peer},
            device_id_type=MESH,
        )
        sent[q, i].start()

    def first(q):
        if q >= 4:
            src = gpiece.at[q - 4]
        else:
            src = piece.at[q]
            assemble(q, src)
        for i, peer in enumerate((xp, yp, sib)):
            send(q, i, src, f, peer)
        put[q] = pltpu.make_async_copy(src, view(q, f), put_sem.at[q])
        put[q].start()

    def relay(q):
        sent[q, 0].wait_recv()
        if q % 2 == 0:
            send(q, 3, None, xp, yp)
        send(q, 4, None, xp, sib)
        sent[q, 1].wait_recv()
        if q % 2 == 1:
            send(q, 3, None, yp, xp)
        send(q, 5, None, yp, sib)

    def across(q):
        sent[q, 3].wait_recv()
        send(q, 6, None, diag, sib)

    first(0)
    first(1)
    relay(0)
    first(2)
    relay(1)
    first(3)
    across(0)
    relay(2)
    arrive(6)
    for h in range(2):
        for g in range(gpiece.shape[1]):
            for b in range(per):
                gpiece[h, g, b] = jnp.concatenate(
                    [gheld[s, g, b, h * ghalf : (h + 1) * ghalf, :] for s in range(zs)], axis=1
                )
    first(4)
    first(5)
    relay(4)
    relay(5)
    assemble(4, piece2.at[pl.ds(0, half)])
    across(1)
    relay(3)
    assemble(5, piece2.at[pl.ds(half, half)])
    for q in (4, 5, 2, 3):
        across(q)
    for q in (4, 5):
        for i in (2, 4, 5, 6):
            sent[q, i].wait_recv()
        put[q].wait()
    for g in range(gfull.shape[0]):
        for b in range(per):
            gates_out[g, b] = gfull[g, b].T
    for q in range(4):
        for i in (2, 4, 5, 6):
            sent[q, i].wait_recv()
        put[q].wait()
    for q in range(6):
        for i in range(7):
            sent[q, i].wait_send()
    for q in range(7):
        for k in range(1, zs):
            a2a[q, k].wait_send()


def spread(groups, gates, zs, fs):
    blocks, chan, rows = groups[0].shape
    kinds, _, gin, gout = gates.shape
    per = blocks // zs
    width = per * chan * zs
    full = jax.ShapeDtypeStruct((rows * fs, width), jnp.bfloat16)
    square = (kinds, per, gin * fs, gout * zs)
    vmem = pl.BlockSpec(memory_space=pltpu.VMEM)
    hbm = pl.BlockSpec(memory_space=pl.ANY)
    dma = pltpu.SemaphoreType.DMA
    return pl.pallas_call(
        spread_body,
        in_specs=[vmem] * 4,
        out_specs=[hbm, hbm, vmem, vmem],
        out_shape=[
            full,
            full,
            jax.ShapeDtypeStruct((rows, width), jnp.bfloat16),
            jax.ShapeDtypeStruct((kinds, per, gout * zs, gin * fs), jnp.bfloat16),
        ],
        scratch_shapes=[
            pltpu.VMEM((3, zs, per, chan, rows), jnp.bfloat16),
            pltpu.VMEM((4, rows // 2, width), jnp.bfloat16),
            pltpu.VMEM((zs, kinds, per, gin, gout), jnp.bfloat16),
            pltpu.VMEM((2, kinds, per, gin // 2, gout * zs), jnp.bfloat16),
            pltpu.VMEM(square, jnp.bfloat16),
            dma((7,)),
            dma((7, zs)),
            dma((7, zs)),
            dma((6,)),
            dma((6, 7)),
            dma((6, 7)),
        ],
        compiler_params=pltpu.CompilerParams(collective_id=0, has_side_effects=True),
        name="spread",
    )(*groups, gates)


def dup_body(x_ref, o_ref):
    o_ref[...] = x_ref[...]


def dup(x):
    rows, width = x.shape
    tile = min(rows, 512)
    spec = pl.BlockSpec((tile, width), lambda i: (i, 0))
    return pl.pallas_call(
        dup_body,
        grid=(rows // tile,),
        in_specs=[spec],
        out_specs=spec,
        out_shape=jax.ShapeDtypeStruct(x.shape, x.dtype),
        cost_estimate=pl.CostEstimate(flops=0, bytes_accessed=4 * rows * width, transcendentals=0),
        name="dup",
    )(x)


def on_device(
    tokens, input_source, branch_source, output_source, gates_source, decay_param, block_order
):
    tensor_count = lax.axis_size("tensor")
    per_dev = block_order.shape[0] // tensor_count
    own_blocks = lax.dynamic_slice_in_dim(block_order, lax.axis_index("tensor") * per_dev, per_dev)
    casted = (
        input_source.astype(jnp.bfloat16),
        branch_source.astype(jnp.bfloat16),
        output_source.astype(jnp.bfloat16),
    )
    gate_cast = gates_source.astype(jnp.bfloat16)
    sectioned = tuple((jnp.take(weight, block_order, axis=1, mode="clip") for weight in casted))
    gate_sectioned = jnp.take(gate_cast, block_order, axis=1, mode="clip")
    row_count = tokens.shape[0]
    if lax.axis_size("fsdp") == 8:
        groups = [jnp.transpose(weight, (1, 0, 2)) for weight in sectioned]
        input_serve, branch_serve, output_piece, gates_serve = spread(
            groups, gate_sectioned, tensor_count, 8
        )
    else:
        gate_group = lax.all_to_all(gate_sectioned, "tensor", split_axis=1, concat_axis=3, tiled=True)
        gate_piece = jnp.transpose(gate_group, (0, 1, 3, 2))
        gates_serve = lax.all_gather(gate_piece, "fsdp", axis=3, tiled=True)
        regrouped = lax.all_to_all(sectioned, "tensor", split_axis=1, concat_axis=0, tiled=True)
        pieces = tuple(
            (jnp.transpose(weight, (2, 1, 0)).reshape(weight.shape[2], -1) for weight in regrouped)
        )
        input_serve = lax.all_gather(pieces[0], "fsdp", axis=0, tiled=True)
        branch_serve = lax.all_gather(pieces[1], "fsdp", axis=0, tiled=True)
        output_piece = pieces[2]
    output_serve = lax.all_gather(output_piece, "fsdp", axis=0, tiled=True)
    rate = -8.0 * jax.nn.softplus(jnp.take(decay_param, own_blocks, axis=0, mode="clip"))[:, None, :]
    branch_in = jnp.dot(tokens, input_serve, preferred_element_type=jnp.float32).astype(jnp.bfloat16)
    gate_pre = jnp.dot(tokens, branch_serve, preferred_element_type=jnp.float32)
    gated = recur(branch_in, gate_pre, gates_serve, rate, row_count // LEN)
    partial_value = lax.dot_general(
        gated, output_serve, (((1,), (1,)), ((), ())), preferred_element_type=jnp.float32
    )
    mixed = lax.psum_scatter(
        partial_value.astype(jnp.bfloat16), "tensor", scatter_dimension=1, tiled=True
    )
    return (mixed, dup(input_serve), dup(branch_serve), dup(output_serve), gates_serve)


def solution(mesh):
    return jax.shard_map(
        on_device,
        mesh=mesh,
        in_specs=(
            P("fsdp", None),
            P("tensor", None, "fsdp"),
            P("tensor", None, "fsdp"),
            P("tensor", None, "fsdp"),
            P(None, None, "fsdp", "tensor"),
            P(),
            P(),
        ),
        out_specs=(
            P("fsdp", "tensor"),
            P(None, "tensor"),
            P(None, "tensor"),
            P(None, "tensor"),
            P(None, "tensor", None, None),
        ),
        check_vma=False,
    )
```
